32 devices in a mesh: cfg: 2 (over y), ta: 8 (over z, x), sa: 2 (over core).
Axes of the slice: x: 2, y: 2, z: 4, core: 2. Of those that a mesh axis runs over, the one named last changes fastest.
Arguments:
- forward: bfloat16 [32, 2, 256, 2, 256], P(('cfg', 'ta'), 'sa'), parts along dimension 0, may hold values from -6 to 6
- backward: bfloat16 [4, 16, 256, 2, 256], P(('cfg', 'sa'), 'ta'), parts along dimension 0, may hold values from -6 to 6
- sink_bank: bfloat16 [32, 9, 256, 2, 256], P(('cfg', 'ta'), None, 'sa'), parts along dimension 0, may hold values from -0.25 to 0.25
- source_bank: bfloat16 [4, 9, 256, 2, 256], P(('cfg', 'sa'), None, 'ta'), parts along dimension 0, may hold values from -0.25 to 0.25
- op_mom: int32 [4], replicated, may hold values from 0 to 2
- op_disp: int32 [4], replicated, may hold values from 0 to 2
Outputs:
- correlator: float32 [32, 2, 2, 4, 4], P(('cfg', 'ta'), 'sa'), parts along dimension 0
The draws below stay inside these ranges and needn't reach their ends.
There are 2 independent parts, one for each index of `cfg`. The reference program is written for one: setup_inputs(seed, part) draws one part's arguments, and reference() takes and returns one part's arrays. A program takes and returns all parts, laid end to end along the dimension named above; an argument that names none is the same for every part. Nothing has to cross between parts.
All inputs are finite; a program needn't handle non-finite values.
Results may differ from the reference program's by a relative error of at most 0.0029.
Values may be sent and summed in bfloat16 or wider, within the bound.
A program may use at most 64 MiB of HBM per device.

```python
import jax
import jax.numpy as jnp
from jax import lax

P_SIZE = 256
NOP = 4
NMOM = 3
NDISP = 3
NBANK = 9
NT = 16
NS = 2


def place_ends(values, own_key, low, largest):
    index_at = [jax.random.randint(jax.random.fold_in(own_key, axis), (), 0, length) for axis, length in enumerate(values.shape)]
    main_axis = values.shape.index(max(values.shape))
    neighbour = index_at[:main_axis] + [(index_at[main_axis] + 1) % values.shape[main_axis]] + index_at[main_axis + 1:]
    return values.at[tuple(index_at)].set(low).at[tuple(neighbour)].set(largest)


def level_of(stream_key, shape, shards, low, high):
    factor_of = 1.0
    for axis_at, shards_of in shards:
        draws = jax.random.uniform(jax.random.fold_in(jax.random.fold_in(stream_key, 6), axis_at), (shards_of,), jnp.float32, low / len(shards), high / len(shards))
        factor_of = factor_of * jnp.repeat(jnp.exp(draws), shape[axis_at] // shards_of).reshape((-1,) + (1,) * (len(shape) - 1 - axis_at))
    return factor_of


def normal_values(stream_key, shape, width, limit, cuts=(), kind=jnp.bfloat16):
    array = jax.random.normal(stream_key, shape, jnp.float32) * width
    if len(cuts) > 0:
        array = level_of(stream_key, shape, cuts, -0.22, 0.18) * array
    return jnp.clip(array, min=-limit, max=limit).astype(kind)


def setup_inputs(seed: int = 0, part: int = 0) -> dict:
    key_of = jax.random.split(jax.random.key(seed), 7)
    part_splits = jax.random.split(jax.random.fold_in(key_of[6], part), 7)
    return {
        "forward": normal_values(part_splits[0], (NT, NS, P_SIZE, 2, P_SIZE), 1.0, 6.0, ((0, 8), (1, 2))),
        "backward": normal_values(part_splits[1], (NS, NT, P_SIZE, 2, P_SIZE), 1.0, 6.0, ((0, 2), (1, 8))),
        "sink_bank": normal_values(part_splits[2], (NT, NBANK, P_SIZE, 2, P_SIZE), (2 * P_SIZE) ** -0.5, 0.25, ((0, 8), (2, 2))),
        "source_bank": normal_values(part_splits[3], (NS, NBANK, P_SIZE, 2, P_SIZE), (2 * P_SIZE) ** -0.5, 0.25, ((0, 2), (2, 8))),
        "op_mom": place_ends(jax.random.randint(key_of[4], (NOP,), 0, NMOM), jax.random.fold_in(key_of[4], 1), 0, NMOM - 1).astype(jnp.int32),
        "op_disp": place_ends(jax.random.randint(key_of[5], (NOP,), 0, NDISP), jax.random.fold_in(key_of[5], 1), 0, NDISP - 1).astype(jnp.int32),
    }


def complex_product(left, right):
    count = left.shape[0]
    height = left.shape[1]
    left_real = left[:, :, 0, :].reshape(count * height, -1)
    left_imag = left[:, :, 1, :].reshape(count * height, -1)
    right_real = right[:, 0, :]
    right_imag = right[:, 1, :]
    real_part = jnp.dot(left_real, right_real, preferred_element_type=jnp.float32) - jnp.dot(left_imag, right_imag, preferred_element_type=jnp.float32)
    imag_part = jnp.dot(left_real, right_imag, preferred_element_type=jnp.float32) + jnp.dot(left_imag, right_real, preferred_element_type=jnp.float32)
    return jnp.stack([real_part, imag_part], axis=1).reshape(count, height, 2, -1)


def reference(forward, backward, sink_bank, source_bank, op_mom, op_disp):
    wanted = (op_mom * NDISP + op_disp).astype(jnp.int32)
    sink_ops = jnp.take(sink_bank, wanted, axis=1)
    source_ops = jnp.take(source_bank, wanted, axis=1)
    back_by_time = jnp.swapaxes(backward, 0, 1)

    def one_time(items):
        ops_here, forward_here, back_here = items
        blocks = []
        for source in range(NS):
            product = complex_product(ops_here, forward_here[source]).astype(jnp.bfloat16)
            reverse = complex_product(source_ops[source], back_here[source])
            paired = jnp.einsum("aicj,bjdi->abcd", product.astype(jnp.float32), reverse, precision=lax.Precision.HIGHEST)
            real_trace = paired[:, :, 0, 0] - paired[:, :, 1, 1]
            imag_trace = paired[:, :, 0, 1] + paired[:, :, 1, 0]
            blocks.append(jnp.stack([real_trace, imag_trace], axis=0) / P_SIZE)
        return jnp.stack(blocks, axis=0)

    return lax.map(one_time, (sink_ops, forward, back_by_time))
```

```python
import functools

import jax
import jax.numpy as jnp
from jax import lax
from jax.experimental import pallas as pl
from jax.experimental.pallas import tpu as pltpu
from jax.sharding import PartitionSpec as P

NDISP = 3
STRIP = 16
LANES = 128
F32 = jnp.float32
BF16 = jnp.bfloat16
MESH = pl.DeviceIdType.MESH


def split_parts(block):
    return pltpu.einshape("rpc->prc", block)


def dot_nt(left, right):
    return lax.dot_general(left, right, (((1,), (1,)), ((), ())), preferred_element_type=F32)


def kernel(gather, groups, mom, disp, fwd_hbm, back_hbm, sink_hbm, source_hbm, out, fwd, back, bank, src_bank,
           ops, left_mat, right_mat, prod, turned, source, acc, in_sem, s_send, s_recv, z_send, z_recv, x_send, x_recv):
    times, nop = ops.shape[0], ops.shape[1]
    half = bank.shape[2]
    size = fwd.shape[1]
    blocks, rows = source.shape[0], source.shape[3]
    sa = lax.axis_index("sa")
    me = lax.axis_index("ta")
    group, side = me // 2, lax.rem(me, 2)
    peers = [lax.rem(group + d, groups) * 2 + side for d in range(1, groups)] if gather else []
    origins = [lax.rem(group - d + groups, groups) * 2 + side for d in range(1, groups)] if gather else []
    cross = group * 2 + 1 - side

    loads = []
    for k, (a, b) in enumerate([(source_hbm, src_bank), (sink_hbm, bank), (fwd_hbm, fwd), (back_hbm, back)]):
        loads.append(pltpu.make_async_copy(a, b, in_sem.at[k]))
        loads[-1].start()

    barrier = pltpu.get_barrier_semaphore()
    pl.semaphore_signal(barrier, inc=1, device_id={"sa": 1 - sa}, device_id_type=MESH)
    if gather:
        for peer in peers + [cross]:
            pl.semaphore_signal(barrier, inc=1, device_id={"ta": peer}, device_id_type=MESH)

    index = [mom[a] * NDISP + disp[a] for a in range(nop)]
    loads[0].wait()
    if gather:
        for b in range(nop):
            source[me, b] = split_parts(src_bank[0, index[b]])
    pl.semaphore_wait(barrier, 1 + len(peers) + (1 if gather else 0))

    sends = []

    def send_source(block, b, target, send_sem, recv_sem):
        copy = pltpu.make_async_remote_copy(
            src_ref=source.at[block, b], dst_ref=source.at[block, b], send_sem=send_sem, recv_sem=recv_sem,
            device_id={"ta": target}, device_id_type=MESH)
        copy.start()
        sends.append(copy)

    if gather:
        for b in range(nop):
            send_source(me, b, cross, x_send.at[0, b], x_recv.at[0, b])
            for d in range(1, groups):
                send_source(me, b, peers[d - 1], z_send.at[d - 1, b], z_recv.at[d - 1, b])

    mine = pl.ds(pl.multiple_of(sa * half, half), half)
    loads[1].wait()
    swaps = []
    for t in range(times):
        for a in range(nop):
            parts = split_parts(bank[t, index[a]])
            for p in range(2):
                ops[t, a, mine, p * size:(p + 1) * size] = parts[p]
    for t in range(times):
        swaps.append(pltpu.make_async_remote_copy(
            src_ref=ops.at[t, :, mine], dst_ref=ops.at[t, :, mine], send_sem=s_send.at[t], recv_sem=s_recv.at[t],
            device_id={"sa": 1 - sa}, device_id_type=MESH))
        swaps[-1].start()

    loads[2].wait()
    for t in range(times):
        parts = split_parts(fwd[t])
        real, imag = parts[0].T, parts[1].T
        left_mat[t, :size, :size] = real
        left_mat[t, :size, size:] = -imag
        left_mat[t, size:, :size] = imag
        left_mat[t, size:, size:] = real
    loads[3].wait()
    for t in range(times):
        parts = split_parts(back[t])
        right_mat[t, :size, :size] = parts[0]
        right_mat[t, :size, size:] = -parts[1]
        right_mat[t, size:, :size] = parts[1]
        right_mat[t, size:, size:] = parts[0]

    acc[...] = jnp.zeros_like(acc)

    def arrived(recv_sem, block, b):
        pltpu.make_async_copy(source.at[block, b], source.at[block, b], recv_sem).wait()

    relays = [(d, b) for b in range(nop) for d in range(1, groups)] if gather else []

    def relay(count):
        for _ in range(min(count, len(relays))):
            d, b = relays.pop(0)
            arrived(z_recv.at[d - 1, b], origins[d - 1], b)
            send_source(origins[d - 1], b, cross, x_send.at[d, b], x_recv.at[d, b])

    for t in range(times):
        swaps[t].wait()
        for a in range(nop):
            result = dot_nt(left_mat[t], ops[t, a]).astype(BF16)
            prod[a, :, :size] = result[:size]
            prod[a, :, size:] = result[size:]
            if t > 0:
                relay(1)
        for a in range(nop):
            turned[t, a] = dot_nt(prod[a], right_mat[t])
            relay(1)

    def contract(block):
        for t in range(times):
            def strip(k, carry):
                carry = list(carry)
                row = pl.multiple_of(k * STRIP, STRIP)
                here = pl.ds(pl.multiple_of(block * rows + k * STRIP, STRIP), STRIP)
                for lane in range(0, size, LANES):
                    ts = [[source[block, b, p, pl.ds(row, STRIP), lane:lane + LANES].astype(F32) for p in range(2)]
                          for b in range(nop)]
                    for a in range(nop):
                        wr = turned[t, a, here, lane:lane + LANES]
                        wi = turned[t, a, here, size + lane:size + lane + LANES]
                        for b in range(nop):
                            tr, ti = ts[b]
                            re = wr * tr - wi * ti
                            im = wr * ti + wi * tr
                            at = a * nop + b
                            carry[at] = carry[at] + (re[:8] + re[8:])
                            carry[nop * nop + at] = carry[nop * nop + at] + (im[:8] + im[8:])
                return tuple(carry)

            start = tuple(acc[t, j] for j in range(2 * nop * nop))
            done = lax.fori_loop(0, rows // STRIP, strip, start)
            for j in range(2 * nop * nop):
                acc[t, j] = done[j]

    if gather:
        contract(me)
        relay(len(relays))
        for d in range(1, groups):
            contract(origins[d - 1])
        for d in range(groups):
            block = cross if d == 0 else lax.rem(group - d + groups, groups) * 2 + 1 - side
            for b in range(nop):
                arrived(x_recv.at[d, b], block, b)
            contract(block)
        for copy in sends:
            copy.wait_send()
    else:
        for k in range(blocks):
            source[k] = src_bank[k]
        lax.fori_loop(0, blocks, lambda k, c: (contract(k), c)[1], 0)

    for t in range(times):
        total = jnp.sum(jnp.sum(acc[t], axis=1), axis=1, keepdims=True) / size
        out[t] = jnp.broadcast_to(total, out.shape[1:])


def per_device(peers, forward, backward, sink_bank, source_bank, op_mom, op_disp):
    times, size = forward.shape[0], forward.shape[2]
    half, nop = sink_bank.shape[2], op_mom.shape[0]
    rows = source_bank.shape[2]
    gather = rows % STRIP == 0 and peers % 2 == 0 and peers > 2
    groups = peers // 2 if gather else 2
    blocks = peers
    if not gather:
        chosen = jnp.take(source_bank[0], op_mom * NDISP + op_disp, axis=0)
        chosen = lax.all_gather(chosen, "ta", axis=1, tiled=True)
        blocks, rows = size // STRIP, STRIP
        source_bank = chosen.reshape(nop, blocks, rows, 2, size).transpose(1, 0, 3, 2, 4)
    smem = pl.BlockSpec(memory_space=pltpu.SMEM)
    hbm = pl.BlockSpec(memory_space=pl.ANY)
    dma = pltpu.SemaphoreType.DMA
    result = pl.pallas_call(
        functools.partial(kernel, gather, groups),
        out_shape=jax.ShapeDtypeStruct((times, 2 * nop * nop, LANES), F32),
        in_specs=[smem, smem, hbm, hbm, hbm, hbm],
        out_specs=pl.BlockSpec(memory_space=pltpu.VMEM),
        scratch_shapes=[
            pltpu.VMEM((times, size, 2, size), BF16),
            pltpu.VMEM((times, size, 2, size), BF16),
            pltpu.VMEM(sink_bank.shape, BF16),
            pltpu.VMEM(source_bank.shape, BF16),
            pltpu.VMEM((times, nop, size, 2 * size), BF16),
            pltpu.VMEM((times, 2 * size, 2 * size), BF16),
            pltpu.VMEM((times, 2 * size, 2 * size), BF16),
            pltpu.VMEM((nop, size, 2 * size), BF16),
            pltpu.VMEM((times, nop, size, 2 * size), F32),
            pltpu.VMEM((blocks, nop, 2, rows, size), BF16),
            pltpu.VMEM((times, 2 * nop * nop, 8, LANES), F32),
            dma((4,)),
            dma((times,)),
            dma((times,)),
            dma((groups - 1, nop)),
            dma((groups - 1, nop)),
            dma((groups, nop)),
            dma((groups, nop)),
        ],
        compiler_params=pltpu.CompilerParams(collective_id=0, has_side_effects=True, vmem_limit_bytes=48 << 20),
    )(op_mom, op_disp, forward[:, 0], backward[0], sink_bank, source_bank)
    return result[:, :, 0].reshape(times, 1, 2, nop, nop)


def solution(mesh):
    placed = (
        P(("cfg", "ta"), "sa", None, None, None),
        P(("cfg", "sa"), "ta", None, None, None),
        P(("cfg", "ta"), None, "sa", None, None),
        P(("cfg", "sa"), None, "ta", None, None),
        P(),
        P(),
    )
    return jax.shard_map(
        functools.partial(per_device, mesh.shape["ta"]),
        mesh=mesh,
        in_specs=placed,
        out_specs=P(("cfg", "ta"), "sa", None, None, None),
        check_vma=False,
    )
```

```python
import functools

import jax
import jax.numpy as jnp
from jax import lax
from jax.experimental import pallas as pl
from jax.experimental.pallas import tpu as pltpu
from jax.sharding import PartitionSpec as P

NDISP = 3
STRIP = 16
LANES = 128
F32 = jnp.float32
BF16 = jnp.bfloat16
MESH = pl.DeviceIdType.MESH


def split_parts(block):
    return pltpu.einshape("rpc->prc", block)


def dot_nt(left, right):
    return lax.dot_general(left, right, (((1,), (1,)), ((), ())), preferred_element_type=F32)


def kernel(gather, groups, mom, disp, fwd_hbm, back_hbm, sink_hbm, source_hbm, out, fwd, back, bank, src_bank,
           ops, left_mat, right_mat, prod, turned, source, acc, in_sem, s_send, s_recv, z_send, z_recv, x_send, x_recv):
    times, nop = ops.shape[0], ops.shape[1]
    half = bank.shape[2]
    size = fwd.shape[1]
    blocks, rows = source.shape[0], source.shape[3]
    sa = lax.axis_index("sa")
    me = lax.axis_index("ta")
    group, side = me // 2, lax.rem(me, 2)
    peers = [lax.rem(group + d, groups) * 2 + side for d in range(1, groups)] if gather else []
    origins = [lax.rem(group - d + groups, groups) * 2 + side for d in range(1, groups)] if gather else []
    cross = group * 2 + 1 - side

    loads = []
    for k, (a, b) in enumerate([(source_hbm, src_bank), (sink_hbm, bank), (fwd_hbm, fwd), (back_hbm, back)]):
        loads.append(pltpu.make_async_copy(a, b, in_sem.at[k]))
        loads[-1].start()

    barrier = pltpu.get_barrier_semaphore()
    pl.semaphore_signal(barrier, inc=1, device_id={"sa": 1 - sa}, device_id_type=MESH)
    if gather:
        for peer in peers + [cross]:
            pl.semaphore_signal(barrier, inc=1, device_id={"ta": peer}, device_id_type=MESH)

    index = [mom[a] * NDISP + disp[a] for a in range(nop)]
    loads[0].wait()
    if gather:
        for b in range(nop):
            source[me, b] = split_parts(src_bank[0, index[b]])
    pl.semaphore_wait(barrier, 1 + len(peers) + (1 if gather else 0))

    sends = []

    def send_source(block, b, target, send_sem, recv_sem):
        copy = pltpu.make_async_remote_copy(
            src_ref=source.at[block, b], dst_ref=source.at[block, b], send_sem=send_sem, recv_sem=recv_sem,
            device_id={"ta": target}, device_id_type=MESH)
        copy.start()
        sends.append(copy)

    if gather:
        for b in range(nop):
            send_source(me, b, cross, x_send.at[0, b], x_recv.at[0, b])
            for d in range(1, groups):
                send_source(me, b, peers[d - 1], z_send.at[d - 1, b], z_recv.at[d - 1, b])

    mine = pl.ds(pl.multiple_of(sa * half, half), half)
    loads[1].wait()
    swaps = []
    for t in range(times):
        for a in range(nop):
            parts = split_parts(bank[t, index[a]])
            for p in range(2):
                ops[t, a, mine, p * size:(p + 1) * size] = parts[p]
    for t in range(times):
        swaps.append(pltpu.make_async_remote_copy(
            src_ref=ops.at[t, :, mine], dst_ref=ops.at[t, :, mine], send_sem=s_send.at[t], recv_sem=s_recv.at[t],
            device_id={"sa": 1 - sa}, device_id_type=MESH))
        swaps[-1].start()

    loads[2].wait()
    for t in range(times):
        parts = split_parts(fwd[t])
        real, imag = parts[0].T, parts[1].T
        left_mat[t, :size, :size] = real
        left_mat[t, :size, size:] = -imag
        left_mat[t, size:, :size] = imag
        left_mat[t, size:, size:] = real
    loads[3].wait()
    for t in range(times):
        parts = split_parts(back[t])
        right_mat[t, :size, :size] = parts[0]
        right_mat[t, :size, size:] = -parts[1]
        right_mat[t, size:, :size] = parts[1]
        right_mat[t, size:, size:] = parts[0]

    acc[...] = jnp.zeros_like(acc)

    def arrived(recv_sem, block, b):
        pltpu.make_async_copy(source.at[block, b], source.at[block, b], recv_sem).wait()

    relays = [(d, b) for b in range(nop) for d in range(1, groups)] if gather else []

    def relay(count):
        for _ in range(min(count, len(relays))):
            d, b = relays.pop(0)
            arrived(z_recv.at[d - 1, b], origins[d - 1], b)
            send_source(origins[d - 1], b, cross, x_send.at[d, b], x_recv.at[d, b])

    for t in range(times):
        swaps[t].wait()
        for a in range(nop):
            result = dot_nt(left_mat[t], ops[t, a]).astype(BF16)
            prod[a, :, :size] = result[:size]
            prod[a, :, size:] = result[size:]
            if t > 0:
                relay(1)
        for a in range(nop):
            turned[t, a] = dot_nt(prod[a], right_mat[t])
            relay(1)

    def contract(block):
        for t in range(times):
            def strip(k, carry):
                carry = list(carry)
                row = pl.multiple_of(k * STRIP, STRIP)
                here = pl.ds(pl.multiple_of(block * rows + k * STRIP, STRIP), STRIP)
                for lane in range(0, size, LANES):
                    ts = [[source[block, b, p, pl.ds(row, STRIP), lane:lane + LANES].astype(F32) for p in range(2)]
                          for b in range(nop)]
                    for a in range(nop):
                        wr = turned[t, a, here, lane:lane + LANES]
                        wi = turned[t, a, here, size + lane:size + lane + LANES]
                        for b in range(nop):
                            tr, ti = ts[b]
                            re = wr * tr - wi * ti
                            im = wr * ti + wi * tr
                            at = 2 * nop * b + a
                            carry[at] = carry[at] + (re[:8] + re[8:])
                            carry[nop + at] = carry[nop + at] + (im[:8] + im[8:])
                return tuple(carry)

            start = tuple(acc[t, j] for j in range(2 * nop * nop))
            done = lax.fori_loop(0, rows // STRIP, strip, start)
            for j in range(2 * nop * nop):
                acc[t, j] = done[j]

    if gather:
        contract(me)
        relay(len(relays))
        for d in range(1, groups):
            contract(origins[d - 1])
        for d in range(groups):
            block = cross if d == 0 else lax.rem(group - d + groups, groups) * 2 + 1 - side
            for b in range(nop):
                arrived(x_recv.at[d, b], block, b)
            contract(block)
        for copy in sends:
            copy.wait_send()
    else:
        for k in range(blocks):
            source[k] = src_bank[k]
        lax.fori_loop(0, blocks, lambda k, c: (contract(k), c)[1], 0)

    for t in range(times):
        total = jnp.sum(jnp.sum(acc[t], axis=1), axis=1, keepdims=True) / size
        lane = lax.broadcasted_iota(jnp.int32, (2 * nop, LANES), 1)
        placed = jnp.zeros((2 * nop, LANES), F32)
        for b in range(nop):
            placed = jnp.where(lane == b, total[2 * nop * b:2 * nop * (b + 1)], placed)
        for c in range(2):
            out[t, c] = placed[nop * c:nop * (c + 1)]


def per_device(peers, forward, backward, sink_bank, source_bank, op_mom, op_disp):
    times, size = forward.shape[0], forward.shape[2]
    half, nop = sink_bank.shape[2], op_mom.shape[0]
    rows = source_bank.shape[2]
    gather = rows % STRIP == 0 and peers % 2 == 0 and peers > 2
    groups = peers // 2 if gather else 2
    blocks = peers
    if not gather:
        chosen = jnp.take(source_bank[0], op_mom * NDISP + op_disp, axis=0)
        chosen = lax.all_gather(chosen, "ta", axis=1, tiled=True)
        blocks, rows = size // STRIP, STRIP
        source_bank = chosen.reshape(nop, blocks, rows, 2, size).transpose(1, 0, 3, 2, 4)
    smem = pl.BlockSpec(memory_space=pltpu.SMEM)
    hbm = pl.BlockSpec(memory_space=pltpu.HBM)
    dma = pltpu.SemaphoreType.DMA
    result = pl.pallas_call(
        functools.partial(kernel, gather, groups),
        out_shape=jax.ShapeDtypeStruct((times, 2, nop, LANES), F32),
        in_specs=[smem, smem, hbm, hbm, hbm, hbm],
        out_specs=pl.BlockSpec(memory_space=pltpu.VMEM),
        scratch_shapes=[
            pltpu.VMEM((times, size, 2, size), BF16),
            pltpu.VMEM((times, size, 2, size), BF16),
            pltpu.VMEM(sink_bank.shape, BF16),
            pltpu.VMEM(source_bank.shape, BF16),
            pltpu.VMEM((times, nop, size, 2 * size), BF16),
            pltpu.VMEM((times, 2 * size, 2 * size), BF16),
            pltpu.VMEM((times, 2 * size, 2 * size), BF16),
            pltpu.VMEM((nop, size, 2 * size), BF16),
            pltpu.VMEM((times, nop, size, 2 * size), F32),
            pltpu.VMEM((blocks, nop, 2, rows, size), BF16),
            pltpu.VMEM((times, 2 * nop * nop, 8, LANES), F32),
            dma((4,)),
            dma((times,)),
            dma((times,)),
            dma((groups - 1, nop)),
            dma((groups - 1, nop)),
            dma((groups, nop)),
            dma((groups, nop)),
        ],
        compiler_params=pltpu.CompilerParams(collective_id=0, has_side_effects=True),
    )(op_mom, op_disp, forward[:, 0], backward[0], sink_bank, source_bank)
    return result[:, None, :, :, :nop]


def solution(mesh):
    placed = (
        P(("cfg", "ta"), "sa", None, None, None),
        P(("cfg", "sa"), "ta", None, None, None),
        P(("cfg", "ta"), None, "sa", None, None),
        P(("cfg", "sa"), None, "ta", None, None),
        P(),
        P(),
    )
    return jax.shard_map(
        functools.partial(per_device, mesh.shape["ta"]),
        mesh=mesh,
        in_specs=placed,
        out_specs=P(("cfg", "ta"), "sa", None, None, None),
        check_vma=False,
    )
```

```python
import functools

import jax
import jax.numpy as jnp
from jax import lax
from jax.experimental import pallas as pl
from jax.experimental.pallas import tpu as pltpu
from jax.sharding import PartitionSpec as P

NDISP = 3
STRIP = 16
LANES = 128
F32 = jnp.float32
BF16 = jnp.bfloat16
MESH = pl.DeviceIdType.MESH


def split_parts(block):
    return pltpu.einshape("rpc->prc", block)


def dot_nt(left, right):
    return lax.dot_general(left, right, (((1,), (1,)), ((), ())), preferred_element_type=F32)


def kernel(gather, groups, mom, disp, fwd_hbm, back_hbm, sink_hbm, source_hbm, out, fwd, back, bank, src_bank,
           ops, left_mat, right_mat, prod, turned, source, acc, in_sem, s_send, s_recv, z_send, z_recv, x_send, x_recv):
    times, nop = ops.shape[0], ops.shape[1]
    half = bank.shape[2]
    size = fwd.shape[1]
    blocks, rows = source.shape[0], source.shape[3]
    sa = lax.axis_index("sa")
    me = lax.axis_index("ta")
    group, side = me // 2, lax.rem(me, 2)
    steps = (1, -1)

    def inside(g):
        return jnp.logical_and(g >= 0, g < groups)

    def device(g, s):
        return g * 2 + s

    cross = group * 2 + 1 - side

    loads = []
    for k, (a, b) in enumerate([(source_hbm, src_bank), (sink_hbm, bank), (fwd_hbm, fwd), (back_hbm, back)]):
        loads.append(pltpu.make_async_copy(a, b, in_sem.at[k]))
        loads[-1].start()

    barrier = pltpu.get_barrier_semaphore()
    pl.semaphore_signal(barrier, inc=1, device_id={"sa": 1 - sa}, device_id_type=MESH)
    if gather:
        pl.semaphore_signal(barrier, inc=1, device_id={"ta": cross}, device_id_type=MESH)
        for step in steps:
            @pl.when(inside(group + step))
            def _(step=step):
                pl.semaphore_signal(barrier, inc=1, device_id={"ta": device(group + step, side)}, device_id_type=MESH)

    index = [mom[a] * NDISP + disp[a] for a in range(nop)]
    loads[0].wait()
    if gather:
        for b in range(nop):
            source[me, b] = split_parts(src_bank[0, index[b]])
    greeted = 1
    if gather:
        greeted = 2 + sum(inside(group + step).astype(jnp.int32) for step in steps)
    pl.semaphore_wait(barrier, greeted)

    sends = []

    def send_source(block, b, target, send_sem, recv_sem, when):
        copy = pltpu.make_async_remote_copy(
            src_ref=source.at[block, b], dst_ref=source.at[block, b], send_sem=send_sem, recv_sem=recv_sem,
            device_id={"ta": target}, device_id_type=MESH)
        copy.start()
        sends.append((when, copy))

    def forward_source(block, b, j, step, hop, when):
        @pl.when(when)
        def _():
            send_source(block, b, device(group + step, side), z_send.at[j, hop, b], z_recv.at[j, hop, b], when)

    if gather:
        for b in range(nop):
            send_source(me, b, cross, x_send.at[0, b], x_recv.at[0, b], None)
            for j, step in enumerate(steps):
                forward_source(me, b, j, step, 0, inside(group + step))

    mine = pl.ds(pl.multiple_of(sa * half, half), half)
    loads[1].wait()
    swaps = []
    for t in range(times):
        for a in range(nop):
            parts = split_parts(bank[t, index[a]])
            for p in range(2):
                ops[t, a, mine, p * size:(p + 1) * size] = parts[p]
    for t in range(times):
        swaps.append(pltpu.make_async_remote_copy(
            src_ref=ops.at[t, :, mine], dst_ref=ops.at[t, :, mine], send_sem=s_send.at[t], recv_sem=s_recv.at[t],
            device_id={"sa": 1 - sa}, device_id_type=MESH))
        swaps[-1].start()

    loads[2].wait()
    for t in range(times):
        parts = split_parts(fwd[t])
        real, imag = parts[0].T, parts[1].T
        left_mat[t, :size, :size] = real
        left_mat[t, :size, size:] = -imag
        left_mat[t, size:, :size] = imag
        left_mat[t, size:, size:] = real
    loads[3].wait()
    for t in range(times):
        parts = split_parts(back[t])
        right_mat[t, :size, :size] = parts[0]
        right_mat[t, :size, size:] = -parts[1]
        right_mat[t, size:, :size] = parts[1]
        right_mat[t, size:, size:] = parts[0]

    acc[...] = jnp.zeros_like(acc)

    def arrived(recv_sem, block, b):
        pltpu.make_async_copy(source.at[block, b], source.at[block, b], recv_sem).wait()

    relays = [(hop, b, j) for hop in range(groups - 1) for b in range(nop) for j in range(2)] if gather else []

    def origin(j, hop):
        return group - steps[j] * (hop + 1)

    def relay(count):
        for _ in range(min(count, len(relays))):
            hop, b, j = relays.pop(0)
            came = inside(origin(j, hop))
            block = device(origin(j, hop), side)

            @pl.when(came)
            def _():
                arrived(z_recv.at[j, hop, b], block, b)
                at = 1 + 2 * hop + j
                send_source(block, b, cross, x_send.at[at, b], x_recv.at[at, b], came)
                if hop + 1 < groups - 1:
                    forward_source(block, b, j, steps[j], hop + 1, inside(group + steps[j]))

    for t in range(times):
        swaps[t].wait()
        for a in range(nop):
            result = dot_nt(left_mat[t], ops[t, a]).astype(BF16)
            prod[a, :, :size] = result[:size]
            prod[a, :, size:] = result[size:]
            relay(1)
        for a in range(nop):
            turned[t, a] = dot_nt(prod[a], right_mat[t])
            relay(1)

    def contract(block):
        for t in range(times):
            def strip(k, carry):
                carry = list(carry)
                row = pl.multiple_of(k * STRIP, STRIP)
                here = pl.ds(pl.multiple_of(block * rows + k * STRIP, STRIP), STRIP)
                for lane in range(0, size, LANES):
                    ts = [[source[block, b, p, pl.ds(row, STRIP), lane:lane + LANES].astype(F32) for p in range(2)]
                          for b in range(nop)]
                    for a in range(nop):
                        wr = turned[t, a, here, lane:lane + LANES]
                        wi = turned[t, a, here, size + lane:size + lane + LANES]
                        for b in range(nop):
                            tr, ti = ts[b]
                            re = wr * tr - wi * ti
                            im = wr * ti + wi * tr
                            at = 2 * nop * b + a
                            carry[at] = carry[at] + (re[:8] + re[8:])
                            carry[nop + at] = carry[nop + at] + (im[:8] + im[8:])
                return tuple(carry)

            start = tuple(acc[t, j] for j in range(2 * nop * nop))
            done = lax.fori_loop(0, rows // STRIP, strip, start)
            for j in range(2 * nop * nop):
                acc[t, j] = done[j]

    if gather:
        contract(me)
        for hop in range(groups - 1):
            while relays and relays[0][0] <= hop:
                relay(1)
            for j in range(2):
                relay(2)
                @pl.when(inside(origin(j, hop)))
                def _():
                    contract(device(origin(j, hop), side))
        for hop in range(-1, groups - 1):
            for j in range(2 if hop >= 0 else 1):
                def receive(at, block):
                    for b in range(nop):
                        arrived(x_recv.at[at, b], block, b)
                    contract(block)

                if hop < 0:
                    receive(0, cross)
                else:
                    @pl.when(inside(origin(j, hop)))
                    def _():
                        receive(1 + 2 * hop + j, device(origin(j, hop), 1 - side))
        for when, copy in sends:
            if when is None:
                copy.wait_send()
        for b in range(nop):
            for j, step in enumerate(steps):
                for hop in range(-1, groups - 1):
                    came = inside(origin(j, hop))
                    if hop >= 0:
                        @pl.when(came)
                        def _():
                            at = 1 + 2 * hop + j
                            pltpu.make_async_copy(source.at[me, b], source.at[me, b], x_send.at[at, b]).wait()
                    if hop + 1 < groups - 1:
                        @pl.when(jnp.logical_and(came, inside(group + step)))
                        def _():
                            pltpu.make_async_copy(source.at[me, b], source.at[me, b], z_send.at[j, hop + 1, b]).wait()
    else:
        for k in range(blocks):
            source[k] = src_bank[k]
        lax.fori_loop(0, blocks, lambda k, c: (contract(k), c)[1], 0)

    for t in range(times):
        total = jnp.sum(jnp.sum(acc[t], axis=1), axis=1, keepdims=True) / size
        lane = lax.broadcasted_iota(jnp.int32, (2 * nop, LANES), 1)
        placed = jnp.zeros((2 * nop, LANES), F32)
        for b in range(nop):
            placed = jnp.where(lane == b, total[2 * nop * b:2 * nop * (b + 1)], placed)
        for c in range(2):
            out[t, c] = placed[nop * c:nop * (c + 1)]


def per_device(peers, forward, backward, sink_bank, source_bank, op_mom, op_disp):
    times, size = forward.shape[0], forward.shape[2]
    half, nop = sink_bank.shape[2], op_mom.shape[0]
    rows = source_bank.shape[2]
    gather = rows % STRIP == 0 and peers % 2 == 0 and peers > 2
    groups = peers // 2 if gather else 2
    blocks = peers
    if not gather:
        chosen = jnp.take(source_bank[0], op_mom * NDISP + op_disp, axis=0)
        chosen = lax.all_gather(chosen, "ta", axis=1, tiled=True)
        blocks, rows = size // STRIP, STRIP
        source_bank = chosen.reshape(nop, blocks, rows, 2, size).transpose(1, 0, 3, 2, 4)
    smem = pl.BlockSpec(memory_space=pltpu.SMEM)
    hbm = pl.BlockSpec(memory_space=pltpu.HBM)
    dma = pltpu.SemaphoreType.DMA
    result = pl.pallas_call(
        functools.partial(kernel, gather, groups),
        out_shape=jax.ShapeDtypeStruct((times, 2, nop, LANES), F32),
        in_specs=[smem, smem, hbm, hbm, hbm, hbm],
        out_specs=pl.BlockSpec(memory_space=pltpu.VMEM),
        scratch_shapes=[
            pltpu.VMEM((times, size, 2, size), BF16),
            pltpu.VMEM((times, size, 2, size), BF16),
            pltpu.VMEM(sink_bank.shape, BF16),
            pltpu.VMEM(source_bank.shape, BF16),
            pltpu.VMEM((times, nop, size, 2 * size), BF16),
            pltpu.VMEM((times, 2 * size, 2 * size), BF16),
            pltpu.VMEM((times, 2 * size, 2 * size), BF16),
            pltpu.VMEM((nop, size, 2 * size), BF16),
            pltpu.VMEM((times, nop, size, 2 * size), F32),
            pltpu.VMEM((blocks, nop, 2, rows, size), BF16),
            pltpu.VMEM((times, 2 * nop * nop, 8, LANES), F32),
            dma((4,)),
            dma((times,)),
            dma((times,)),
            dma((2, groups - 1, nop)),
            dma((2, groups - 1, nop)),
            dma((2 * groups - 1, nop)),
            dma((2 * groups - 1, nop)),
        ],
        compiler_params=pltpu.CompilerParams(collective_id=0, has_side_effects=True),
    )(op_mom, op_disp, forward[:, 0], backward[0], sink_bank, source_bank)
    return result[:, None, :, :, :nop]


def solution(mesh):
    placed = (
        P(("cfg", "ta"), "sa", None, None, None),
        P(("cfg", "sa"), "ta", None, None, None),
        P(("cfg", "ta"), None, "sa", None, None),
        P(("cfg", "sa"), None, "ta", None, None),
        P(),
        P(),
    )
    return jax.shard_map(
        functools.partial(per_device, mesh.shape["ta"]),
        mesh=mesh,
        in_specs=placed,
        out_specs=P(("cfg", "ta"), "sa", None, None, None),
        check_vma=False,
    )
```

```python
import functools

import jax
import jax.numpy as jnp
from jax import lax
from jax.experimental import pallas as pl
from jax.experimental.pallas import tpu as pltpu
from jax.sharding import PartitionSpec as P

NDISP = 3
STRIP = 16
LANES = 128
F32 = jnp.float32
BF16 = jnp.bfloat16
MESH = pl.DeviceIdType.MESH


def split_parts(block):
    return pltpu.einshape("rpc->prc", block)


def dot_nt(left, right):
    return lax.dot_general(left, right, (((1,), (1,)), ((), ())), preferred_element_type=F32)


def kernel(gather, groups, mom, disp, fwd_hbm, back_hbm, sink_hbm, source_hbm, out, fwd, back, bank, src_bank,
           ops, left_mat, right_mat, prod, turned, source, acc, in_sem, s_send, s_recv, z_send, z_recv, x_send, x_recv):
    times, nop = ops.shape[0], ops.shape[1]
    half = bank.shape[2]
    size = fwd.shape[1]
    blocks, rows = source.shape[0], source.shape[3]
    sa = lax.axis_index("sa")
    me = lax.axis_index("ta")
    group, side = me // 2, lax.rem(me, 2)
    steps = (1, -1)

    def inside(g):
        return jnp.logical_and(g >= 0, g < groups)

    def device(g, s):
        return g * 2 + s

    cross = group * 2 + 1 - side

    loads = []
    for k, (a, b) in enumerate([(source_hbm, src_bank), (sink_hbm, bank), (fwd_hbm, fwd), (back_hbm, back)]):
        loads.append(pltpu.make_async_copy(a, b, in_sem.at[k]))
        loads[-1].start()

    barrier = pltpu.get_barrier_semaphore()
    pl.semaphore_signal(barrier, inc=1, device_id={"sa": 1 - sa}, device_id_type=MESH)
    if gather:
        pl.semaphore_signal(barrier, inc=1, device_id={"ta": cross}, device_id_type=MESH)
        for step in steps:
            @pl.when(inside(group + step))
            def _(step=step):
                pl.semaphore_signal(barrier, inc=1, device_id={"ta": device(group + step, side)}, device_id_type=MESH)

    index = [mom[a] * NDISP + disp[a] for a in range(nop)]
    loads[0].wait()
    if gather:
        for b in range(nop):
            source[me, b] = split_parts(src_bank[0, index[b]])
    greeted = 1
    if gather:
        greeted = 2 + sum(inside(group + step).astype(jnp.int32) for step in steps)
    pl.semaphore_wait(barrier, greeted)

    sends = []

    def send_source(block, b, target, send_sem, recv_sem, when):
        copy = pltpu.make_async_remote_copy(
            src_ref=source.at[block, b], dst_ref=source.at[block, b], send_sem=send_sem, recv_sem=recv_sem,
            device_id={"ta": target}, device_id_type=MESH)
        copy.start()
        sends.append((when, copy))

    def forward_source(block, b, j, step, hop, when):
        @pl.when(when)
        def _():
            send_source(block, b, device(group + step, side), z_send.at[j, hop, b], z_recv.at[j, hop, b], when)

    if gather:
        for b in range(nop):
            send_source(me, b, cross, x_send.at[0, b], x_recv.at[0, b], None)
            for j, step in enumerate(steps):
                forward_source(me, b, j, step, 0, inside(group + step))

    mine = pl.ds(pl.multiple_of(sa * half, half), half)
    loads[1].wait()
    swaps = []
    for t in range(times):
        for a in range(nop):
            parts = split_parts(bank[t, index[a]])
            for p in range(2):
                ops[t, a, mine, p * size:(p + 1) * size] = parts[p]
    for t in range(times):
        swaps.append(pltpu.make_async_remote_copy(
            src_ref=ops.at[t, :, mine], dst_ref=ops.at[t, :, mine], send_sem=s_send.at[t], recv_sem=s_recv.at[t],
            device_id={"sa": 1 - sa}, device_id_type=MESH))
        swaps[-1].start()

    loads[2].wait()
    for t in range(times):
        parts = split_parts(fwd[t])
        real, imag = parts[0].T, parts[1].T
        left_mat[t, :size, :size] = real
        left_mat[t, :size, size:] = -imag
        left_mat[t, size:, :size] = imag
        left_mat[t, size:, size:] = real
    loads[3].wait()
    for t in range(times):
        parts = split_parts(back[t])
        right_mat[t, :size, :size] = parts[0]
        right_mat[t, :size, size:] = -parts[1]
        right_mat[t, size:, :size] = parts[1]
        right_mat[t, size:, size:] = parts[0]

    acc[...] = jnp.zeros_like(acc)

    def arrived(recv_sem, block, b):
        pltpu.make_async_copy(source.at[block, b], source.at[block, b], recv_sem).wait()

    relays = [(hop, b, j) for hop in range(groups - 1) for b in range(nop) for j in range(2)] if gather else []

    def origin(j, hop):
        return group - steps[j] * (hop + 1)

    def relay(count):
        for _ in range(min(count, len(relays))):
            hop, b, j = relays.pop(0)
            came = inside(origin(j, hop))
            block = device(origin(j, hop), side)

            @pl.when(came)
            def _():
                arrived(z_recv.at[j, hop, b], block, b)
                at = 1 + 2 * hop + j
                send_source(block, b, cross, x_send.at[at, b], x_recv.at[at, b], came)
                if hop + 1 < groups - 1:
                    forward_source(block, b, j, steps[j], hop + 1, inside(group + steps[j]))

    for t in range(times):
        swaps[t].wait()
        for a in range(nop):
            result = dot_nt(left_mat[t], ops[t, a]).astype(BF16)
            prod[a, :, :size] = result[:size]
            prod[a, :, size:] = result[size:]
            if t > 0:
                relay(1)
        for a in range(nop):
            turned[t, a] = dot_nt(prod[a], right_mat[t])
            relay(1)

    def contract(block):
        for t in range(times):
            def strip(k, carry):
                carry = list(carry)
                row = pl.multiple_of(k * STRIP, STRIP)
                here = pl.ds(pl.multiple_of(block * rows + k * STRIP, STRIP), STRIP)
                for lane in range(0, size, LANES):
                    ts = [[source[block, b, p, pl.ds(row, STRIP), lane:lane + LANES].astype(F32) for p in range(2)]
                          for b in range(nop)]
                    for a in range(nop):
                        wr = turned[t, a, here, lane:lane + LANES]
                        wi = turned[t, a, here, size + lane:size + lane + LANES]
                        for b in range(nop):
                            tr, ti = ts[b]
                            re = wr * tr - wi * ti
                            im = wr * ti + wi * tr
                            at = 2 * nop * b + a
                            carry[at] = carry[at] + (re[:8] + re[8:])
                            carry[nop + at] = carry[nop + at] + (im[:8] + im[8:])
                return tuple(carry)

            start = tuple(acc[t, j] for j in range(2 * nop * nop))
            done = lax.fori_loop(0, rows // STRIP, strip, start)
            for j in range(2 * nop * nop):
                acc[t, j] = done[j]

    if gather:
        contract(me)
        for hop in range(groups - 1):
            while relays and relays[0][0] <= hop:
                relay(1)
            for j in range(2):
                relay(2)
                @pl.when(inside(origin(j, hop)))
                def _():
                    contract(device(origin(j, hop), side))
        for hop in range(-1, groups - 1):
            for j in range(2 if hop >= 0 else 1):
                def receive(at, block):
                    for b in range(nop):
                        arrived(x_recv.at[at, b], block, b)
                    contract(block)

                if hop < 0:
                    receive(0, cross)
                else:
                    @pl.when(inside(origin(j, hop)))
                    def _():
                        receive(1 + 2 * hop + j, device(origin(j, hop), 1 - side))
        for when, copy in sends:
            if when is None:
                copy.wait_send()
        for b in range(nop):
            for j, step in enumerate(steps):
                for hop in range(-1, groups - 1):
                    came = inside(origin(j, hop))
                    if hop >= 0:
                        @pl.when(came)
                        def _():
                            at = 1 + 2 * hop + j
                            pltpu.make_async_copy(source.at[me, b], source.at[me, b], x_send.at[at, b]).wait()
                    if hop + 1 < groups - 1:
                        @pl.when(jnp.logical_and(came, inside(group + step)))
                        def _():
                            pltpu.make_async_copy(source.at[me, b], source.at[me, b], z_send.at[j, hop + 1, b]).wait()
    else:
        for k in range(blocks):
            source[k] = src_bank[k]
        lax.fori_loop(0, blocks, lambda k, c: (contract(k), c)[1], 0)

    for t in range(times):
        total = jnp.sum(jnp.sum(acc[t], axis=1), axis=1, keepdims=True) / size
        lane = lax.broadcasted_iota(jnp.int32, (2 * nop, LANES), 1)
        placed = jnp.zeros((2 * nop, LANES), F32)
        for b in range(nop):
            placed = jnp.where(lane == b, total[2 * nop * b:2 * nop * (b + 1)], placed)
        for c in range(2):
            out[t, c] = placed[nop * c:nop * (c + 1)]


def per_device(peers, forward, backward, sink_bank, source_bank, op_mom, op_disp):
    times, size = forward.shape[0], forward.shape[2]
    half, nop = sink_bank.shape[2], op_mom.shape[0]
    rows = source_bank.shape[2]
    gather = rows % STRIP == 0 and peers % 2 == 0 and peers > 2
    groups = peers // 2 if gather else 2
    blocks = peers
    if not gather:
        chosen = jnp.take(source_bank[0], op_mom * NDISP + op_disp, axis=0)
        chosen = lax.all_gather(chosen, "ta", axis=1, tiled=True)
        blocks, rows = size // STRIP, STRIP
        source_bank = chosen.reshape(nop, blocks, rows, 2, size).transpose(1, 0, 3, 2, 4)
    smem = pl.BlockSpec(memory_space=pltpu.SMEM)
    hbm = pl.BlockSpec(memory_space=pltpu.HBM)
    dma = pltpu.SemaphoreType.DMA
    result = pl.pallas_call(
        functools.partial(kernel, gather, groups),
        out_shape=jax.ShapeDtypeStruct((times, 2, nop, LANES), F32),
        in_specs=[smem, smem, hbm, hbm, hbm, hbm],
        out_specs=pl.BlockSpec(memory_space=pltpu.VMEM),
        scratch_shapes=[
            pltpu.VMEM((times, size, 2, size), BF16),
            pltpu.VMEM((times, size, 2, size), BF16),
            pltpu.VMEM(sink_bank.shape, BF16),
            pltpu.VMEM(source_bank.shape, BF16),
            pltpu.VMEM((times, nop, size, 2 * size), BF16),
            pltpu.VMEM((times, 2 * size, 2 * size), BF16),
            pltpu.VMEM((times, 2 * size, 2 * size), BF16),
            pltpu.VMEM((nop, size, 2 * size), BF16),
            pltpu.VMEM((times, nop, size, 2 * size), F32),
            pltpu.VMEM((blocks, nop, 2, rows, size), BF16),
            pltpu.VMEM((times, 2 * nop * nop, 8, LANES), F32),
            dma((4,)),
            dma((times,)),
            dma((times,)),
            dma((2, groups - 1, nop)),
            dma((2, groups - 1, nop)),
            dma((2 * groups - 1, nop)),
            dma((2 * groups - 1, nop)),
        ],
        compiler_params=pltpu.CompilerParams(collective_id=0, has_side_effects=True),
    )(op_mom, op_disp, forward[:, 0], backward[0], sink_bank, source_bank)
    return result[:, None, :, :, :nop]


def solution(mesh):
    placed = (
        P(("cfg", "ta"), "sa", None, None, None),
        P(("cfg", "sa"), "ta", None, None, None),
        P(("cfg", "ta"), None, "sa", None, None),
        P(("cfg", "sa"), None, "ta", None, None),
        P(),
        P(),
    )
    return jax.shard_map(
        functools.partial(per_device, mesh.shape["ta"]),
        mesh=mesh,
        in_specs=placed,
        out_specs=P(("cfg", "ta"), "sa", None, None, None),
        check_vma=False,
    )
```
